128 devices in a mesh: row: 16 (over y, x), col: 8 (over z, core).
Axes of the slice: x: 4, y: 4, z: 4, core: 2. Of those that a mesh axis runs over, the one named last changes fastest.
Arguments:
- front_first: float32 [16, 4, 128, 8, 8, 128], P('row', None, None, 'col'), as said below
- front_second: float32 [16, 4, 128, 8, 8, 128], P('row', None, None, 'col'), as said below
- front_third: float32 [16, 4, 128, 8, 8, 128], P('row', None, None, 'col'), as said below
- map_second: int32 [60], replicated, may hold values from 0 to 63, as said below
- map_third: int32 [60], replicated, may hold values from 0 to 63, as said below
Outputs:
- lower_first: float32 [16, 4, 128, 512], P('row')
- lower_second: float32 [16, 4, 128, 512], P('row')
- lower_third: float32 [16, 4, 128, 512], P('row')
- schur_third: float32 [16, 4, 128, 8, 8, 128], P('row', None, None, 'col')
The draws below stay inside these ranges and needn't reach their ends.
Inputs may be any that keep to these rules, and one draw needn't show every extreme that they name: `map_second`: strictly increasing; the first entry is 0 and the last is 63. `map_third`: strictly increasing; the first entry is 0 and the last is 63. `front_first`: symmetric positive definite. `front_second`: symmetric positive definite. `front_third`: symmetric positive definite.
All inputs are finite; a program needn't handle non-finite values.
Results may differ from the reference program's by a relative error of at most 0.00012.
Values sent between devices are 32-bit elements; how exact they have to be, the bound alone decides.
No kernel may reach another device: no remote copies, remote signals or barrier semaphores. Data moves between devices by JAX's collectives and lax.ppermute only.
A program may use at most 128 MiB of HBM per device.

```python
import math
import jax
import jax.numpy as jnp
from jax import lax

TILE = 128
PANEL = 512
PANELS = 1
FRONT = 8192
GRID_ROWS = 16
GRID_COLS = 8
TILES_ROW = 4
TILES_COL = 8
PIVOTS = 512
BLOCKS = 64
CHILD_BLOCKS = 60


def make_front(key):
    entries = jax.random.normal(key, (FRONT, PIVOTS), jnp.float32)
    factors = entries * (2.0 / math.sqrt(PIVOTS))
    product = jnp.dot(factors, factors.T, precision=lax.Precision.HIGHEST, preferred_element_type=jnp.float32)
    product = 0.5 * (product + product.T)
    diagonal_values = jax.random.uniform(jax.random.fold_in(key, 7), (FRONT,), jnp.float32, 1.0, 2.0)
    matrix = product + jnp.diag(diagonal_values)
    return matrix.reshape(TILES_ROW, GRID_ROWS, TILE, TILES_COL, GRID_COLS, TILE).transpose(1, 0, 2, 4, 3, 5)


def make_map(key):
    pivot_blocks = PIVOTS // TILE
    shuffled = jax.random.permutation(key, BLOCKS - 2) + 1
    skipped = shuffled[:pivot_blocks]
    block_ids = jnp.arange(BLOCKS, dtype=jnp.int32)
    skipped_mask = jnp.any(block_ids[:, None] == skipped[None, :], axis=1)
    ranking = block_ids + BLOCKS * skipped_mask.astype(jnp.int32)
    return jnp.argsort(ranking)[:BLOCKS - pivot_blocks].astype(jnp.int32)


def draw_front_first(key, part):
    return make_front(jax.random.fold_in(key, 1))


def draw_front_second(key, part):
    return make_front(jax.random.fold_in(key, 2))


def draw_front_third(key, part):
    return make_front(jax.random.fold_in(key, 3))


def draw_map_second(key, part):
    return make_map(jax.random.fold_in(key, 11))


def draw_map_third(key, part):
    return make_map(jax.random.fold_in(key, 12))


def setup_inputs(seed: int = 0) -> dict:
    key_of = jax.random.split(jax.random.key(seed), 6)
    front_first = draw_front_first(jax.random.fold_in(key_of[5], 71), 0)
    front_second = draw_front_second(jax.random.fold_in(key_of[5], 71), 0)
    front_third = draw_front_third(jax.random.fold_in(key_of[5], 71), 0)
    map_second = draw_map_second(jax.random.fold_in(key_of[5], 71), 0)
    map_third = draw_map_third(jax.random.fold_in(key_of[5], 71), 0)
    return dict(front_first=front_first, front_second=front_second, front_third=front_third, map_second=map_second, map_third=map_third)


def unpack(front):
    return front.transpose(1, 0, 2, 4, 3, 5).reshape(FRONT, FRONT)

def to_layout(matrix):
    return matrix.reshape(TILES_ROW, GRID_ROWS, TILE, TILES_COL, GRID_COLS, TILE).transpose(1, 0, 2, 4, 3, 5)

def rows_layout(lower_all):
    return lower_all.reshape(TILES_ROW, GRID_ROWS, TILE, PIVOTS).transpose(1, 0, 2, 3)

def factor(matrix):
    row_ids = jnp.arange(FRONT)
    panels = []
    for panel_step in range(PANELS):
        start = panel_step * PANEL
        diagonal = matrix[start:start + PANEL, start:start + PANEL]
        factor_block = jnp.linalg.cholesky(diagonal)
        inverse = lax.linalg.triangular_solve(factor_block, jnp.eye(PANEL, dtype=jnp.float32), left_side=True, lower=True)
        panel_now = jnp.dot(matrix[:, start:start + PANEL].astype(jnp.float32), inverse.T.astype(jnp.float32), precision=lax.Precision.HIGHEST, preferred_element_type=jnp.float32)
        panel_now = jnp.where((row_ids >= start)[:, None], panel_now, 0.0)
        matrix = matrix - jnp.dot(panel_now.astype(jnp.float32), panel_now.T.astype(jnp.float32), precision=lax.Precision.HIGHEST, preferred_element_type=jnp.float32)
        panels.append(panel_now)
    row_keep = row_ids >= PIVOTS
    schur = jnp.where(row_keep[:, None] & row_keep[None, :], matrix, 0.0)
    return (jnp.concatenate(panels, axis=1), schur)

def extend(parent, schur, block_map):
    pivot_blocks = PIVOTS // TILE
    child_tiles = schur.reshape(BLOCKS, TILE, BLOCKS, TILE)[pivot_blocks:, :, pivot_blocks:, :]
    placed_rows = jnp.zeros((BLOCKS, TILE, CHILD_BLOCKS, TILE), schur.dtype).at[block_map].set(child_tiles)
    placed = jnp.zeros((BLOCKS, TILE, BLOCKS, TILE), schur.dtype).at[:, :, block_map, :].set(placed_rows)
    return parent + placed.reshape(FRONT, FRONT)

def reference(front_first, front_second, front_third, map_second, map_third):
    lower_first, schur_first = factor(unpack(front_first))
    lower_second, schur_second = factor(extend(unpack(front_second), schur_first, map_second))
    lower_third, schur_third = factor(extend(unpack(front_third), schur_second, map_third))
    return (rows_layout(lower_first), rows_layout(lower_second), rows_layout(lower_third), to_layout(schur_third))
```

```python
import jax
import jax.numpy as jnp
from jax import lax
from jax.experimental import pallas as pl
from jax.experimental.pallas import tpu as pltpu
from jax.sharding import PartitionSpec as P

TILE = 128
PIVOTS = 512
BLOCKS = 64
ROWS = 16
COLS = 8
TR = 4
TC = 8
MAXD = 4
F32 = jnp.float32
HI = lax.Precision.HIGHEST
BOTH = ("row", "col")


def full(x):
    return jnp.broadcast_to(x, (8, 128))


def base128(tiles, inv):
    sub = lax.broadcasted_iota(jnp.int32, (8, 128), 0)
    n = len(tiles)
    for b in range(n):
        c0 = 8 * b
        rows = tiles[b]
        cols = [full(rows[:, c0 + c : c0 + c + 1]) for c in range(8)]
        e = [[full(cols[c][r : r + 1, :]) for c in range(r + 1)] for r in range(8)]
        low = [[None] * 8 for _ in range(8)]
        s = [None] * 8
        for j in range(8):
            s[j] = lax.rsqrt(e[j][j])
            for i in range(j + 1, 8):
                low[i][j] = e[i][j] * s[j]
            for i in range(j + 1, 8):
                for k in range(j + 1, i + 1):
                    e[i][k] = e[i][k] - low[i][j] * low[k][j]
        w = [[None] * 8 for _ in range(8)]
        for k in range(8):
            w[k][k] = s[k]
            for i in range(k + 1, 8):
                acc = low[i][k] * w[k][k]
                for m in range(k + 1, i):
                    acc = acc + low[i][m] * w[m][k]
                w[i][k] = -(acc * s[i])
        wcol = []
        for k in range(8):
            v = w[7][k]
            for i in range(6, k - 1, -1):
                v = jnp.where(sub == i, w[i][k], v)
            if k > 0:
                v = jnp.where(sub < k, 0.0, v)
            wcol.append(v)

        def apply(x):
            acc = wcol[0] * full(x[0:1, :])
            for k in range(1, 8):
                acc = acc + wcol[k] * full(x[k : k + 1, :])
            return acc

        upper = apply(rows)
        inv[b] = apply(inv[b])
        if b == n - 1:
            break

        def weighted(x):
            parts = [full(x[i : i + 1, :]) for i in range(8)]
            out = []
            for k in range(8):
                acc = w[k][k] * parts[k]
                for i in range(k + 1, 8):
                    acc = acc + w[i][k] * parts[i]
                out.append(acc)
            return out

        zt = weighted(upper)
        zv = weighted(inv[b])
        for r in range(b + 1, n):
            t = tiles[r]
            v = inv[r]
            for k in range(8):
                c = full(tiles[r][:, c0 + k : c0 + k + 1])
                t = t - c * zt[k]
                v = v - c * zv[k]
            tiles[r] = t
            inv[r] = v
    return inv


def kdot(a, b, dims=(((1,), (0,)), ((), ()))):
    return lax.dot_general(a, b, dims, precision=HI, preferred_element_type=F32)


TN = (((0,), (0,)), ((), ()))


def chol_kernel(d_ref, w_ref, a_ref, wk_ref):
    a_ref[...] = d_ref[...]
    w_ref[...] = jnp.zeros((PIVOTS, PIVOTS), F32)
    ri = lax.broadcasted_iota(jnp.int32, (8, 128), 0)
    ci = lax.broadcasted_iota(jnp.int32, (8, 128), 1)

    def body(kb, carry):
        o = pl.multiple_of(kb * 128, 128)
        tiles = [a_ref[pl.ds(o + 8 * r, 8), pl.ds(o, 128)] for r in range(16)]
        inv = [jnp.where(ri + 8 * r == ci, 1.0, 0.0).astype(F32) for r in range(16)]
        inv = base128(tiles, inv)
        for r in range(16):
            wk_ref[8 * r : 8 * r + 8, :] = inv[r]
        for kk in range(4):

            @pl.when(kb == kk)
            def _(kk=kk):
                k0 = kk * 128
                k1 = k0 + 128
                wk = wk_ref[...]
                if kk > 0:
                    w_ref[k0:k1, :k0] = kdot(wk, w_ref[k0:k1, :k0])
                w_ref[k0:k1, k0:k1] = wk
                if kk < 3:
                    u = kdot(wk, a_ref[k0:k1, k1:])
                    a_ref[k1:, k1:] = a_ref[k1:, k1:] - kdot(u, u, TN)
                    w_ref[k1:, :k1] = w_ref[k1:, :k1] - kdot(u, w_ref[k0:k1, :k1], TN)

        return carry

    lax.fori_loop(0, 4, body, 0)


def inverse_factor(d):
    return pl.pallas_call(
        chol_kernel,
        out_shape=jax.ShapeDtypeStruct((PIVOTS, PIVOTS), F32),
        scratch_shapes=[pltpu.VMEM((PIVOTS, PIVOTS), F32), pltpu.VMEM((128, 128), F32)],
        cost_estimate=pl.CostEstimate(
            flops=25_000_000_000, transcendentals=512, bytes_accessed=2_000_000
        ),
        compiler_params=pltpu.CompilerParams(vmem_limit_bytes=32 << 20),
    )(d)


def panel_kernel(c1_ref, c2_ref, k_ref, r1_ref, r2_ref, r3_ref, g_ref, s_ref):
    def row(i, j, t, c):
        return k_ref[i, j, pl.ds(t * 4 + c, 1), :]

    def first(p, carry):
        t = p // ROWS
        i = p % ROWS
        for q in range(4):
            r1_ref[p, q : q + 1, :] = row(i, q, t, 0)
        cp = c1_ref[p]
        cc = jnp.maximum(cp, 0)
        tt = cc // ROWS
        ii = cc % ROWS
        for q in range(8):
            cq = c1_ref[q]
            qq = jnp.maximum(cq, 0)
            got = row(ii, qq % COLS, tt, qq // COLS)
            got = jnp.where((cp >= 0) & (cq >= 0), got, 0.0)
            val = row(i, q, t, 2) + got
            s_ref[p, q : q + 1, :] = val
            if q < 4:
                r2_ref[p, q : q + 1, :] = val
        return carry

    lax.fori_loop(0, BLOCKS, first, 0)

    def second(p, carry):
        t = p // ROWS
        i = p % ROWS
        cp = c2_ref[p]
        cc = jnp.maximum(cp, 0)
        for q in range(4):
            cq = c2_ref[q]
            qq = jnp.maximum(cq, 0)
            got = s_ref[cc, pl.ds(qq, 1), :]
            got = jnp.where((cp >= 0) & (cq >= 0), got, 0.0)
            r3_ref[p, q : q + 1, :] = row(i, q, t, 3) + got
        return carry

    lax.fori_loop(0, BLOCKS, second, 0)
    g_ref[0:4] = r1_ref[0:4]
    g_ref[4:8] = r2_ref[0:4]
    g_ref[20:24] = r3_ref[0:4]
    for q in range(4):
        a = c1_ref[q]
        g_ref[8 + q] = jnp.where(a >= 0, r1_ref[jnp.maximum(a, 0)], 0.0)
        b = c2_ref[q]
        c = c1_ref[jnp.maximum(b, 0)]
        g_ref[12 + q] = jnp.where((b >= 0) & (c >= 0), r1_ref[jnp.maximum(c, 0)], 0.0)
        g_ref[16 + q] = jnp.where(b >= 0, r2_ref[jnp.maximum(b, 0)], 0.0)


def panels(c1, c2, k):
    smem = pl.BlockSpec(memory_space=pltpu.SMEM)
    vmem = pl.BlockSpec(memory_space=pltpu.VMEM)
    return pl.pallas_call(
        panel_kernel,
        out_shape=[jax.ShapeDtypeStruct((BLOCKS, 4, 128), F32)] * 3
        + [jax.ShapeDtypeStruct((24, 4, 128), F32)],
        in_specs=[smem, smem, vmem],
        out_specs=[vmem] * 4,
        scratch_shapes=[pltpu.VMEM((BLOCKS, 8, 128), F32)],
        compiler_params=pltpu.CompilerParams(vmem_limit_bytes=32 << 20),
    )(c1, c2, k)


def extend_kernel(c1_ref, c2_ref, m1_ref, m2_ref, a_ref, f_ref, o_ref, s_ref):
    def moved(src, m_ref, c):
        cc = jnp.maximum(c, 0)
        t = cc // ROWS
        i = cc % ROWS
        x = [src[i, j, t] for j in range(COLS)]
        x = x + [pltpu.roll(x[j], 7, 0) for j in range(MAXD)]
        out = []
        for j in range(COLS):
            acc = m_ref[0, j] * x[j]
            for d in range(1, MAXD + 1):
                acc = acc + m_ref[d, j] * x[j + d]
            out.append(jnp.where(c >= 0, acc, 0.0))
        return out

    def first(p, carry):
        got = moved(a_ref, m1_ref, c1_ref[p])
        t = p // ROWS
        i = p % ROWS
        for j in range(COLS):
            s_ref[i, j, t] = f_ref[i, j, t] + got[j]
        return carry

    lax.fori_loop(0, BLOCKS, first, 0)

    def second(p, carry):
        got = moved(s_ref, m2_ref, c2_ref[p])
        t = p // ROWS
        i = p % ROWS
        for j in range(COLS):
            o_ref[i, j, t] = got[j]
        return carry

    lax.fori_loop(0, BLOCKS, second, 0)


def extended(c1, c2, m1, m2, a, f):
    smem = pl.BlockSpec(memory_space=pltpu.SMEM)
    vmem = pl.BlockSpec(memory_space=pltpu.VMEM)
    shape = (ROWS, COLS, TR, TC, 128)
    return pl.pallas_call(
        extend_kernel,
        out_shape=jax.ShapeDtypeStruct(shape, F32),
        in_specs=[smem, smem, vmem, vmem, vmem, vmem],
        out_specs=vmem,
        scratch_shapes=[pltpu.VMEM(shape, F32)],
        compiler_params=pltpu.CompilerParams(vmem_limit_bytes=32 << 20),
    )(c1, c2, m1, m2, a, f)


def dot(a, b):
    return jnp.dot(a, b, precision=HI, preferred_element_type=F32)


def dot_t(a, b):
    return lax.dot_general(
        a, b, (((1,), (1,)), ((), ())), precision=HI, preferred_element_type=F32
    )


def child_of(block_map):
    blocks = jnp.arange(BLOCKS, dtype=jnp.int32)
    hit = block_map[None, :] == blocks[:, None]
    ids = jnp.arange(block_map.shape[0], dtype=jnp.int32) + (PIVOTS // TILE + 1)
    return jnp.sum(jnp.where(hit, ids[None, :], 0), axis=1) - 1


def column_masks(child):
    blocks = jnp.arange(BLOCKS, dtype=jnp.int32)
    hits = jnp.stack([child == blocks + d for d in range(MAXD + 1)])
    hits = hits.reshape(MAXD + 1, TC, COLS).transpose(0, 2, 1).astype(F32)
    return jnp.broadcast_to(hits[..., None], (MAXD + 1, COLS, TC, 128))


def one_hot(child):
    return (child[:, None] == jnp.arange(BLOCKS, dtype=jnp.int32)[None, :]).astype(F32)


def to_all(rows):
    n = rows.shape[0]
    many = jnp.broadcast_to(rows[None], (128, n, PIVOTS))
    return lax.all_to_all(many, BOTH, 0, 0, tiled=True).transpose(1, 0, 2)


def per_device(front_first, front_second, front_third, map_second, map_third):
    first = front_first.reshape(TR, TILE, TC, TILE)
    second = front_second.reshape(TR, TILE, TC, TILE)
    third = front_third.reshape(TR, TILE, TC, TILE)
    c1 = child_of(map_second)
    c2 = child_of(map_third)
    e1 = one_hot(c1)
    e2 = one_hot(c2)

    packed = jnp.concatenate([first[:, :, 0:2], second[:, :, 0:1], third[:, :, 0:1]], axis=2)
    packed = packed.transpose(1, 0, 2, 3).reshape(128, 16, 128)
    packed = lax.all_to_all(packed, BOTH, 0, 0, tiled=True).reshape(ROWS, COLS, 16, 128)
    r1, r2, r3, g = panels(c1, c2, packed)
    r1, r2, r3 = (r.reshape(BLOCKS, PIVOTS) for r in (r1, r2, r3))
    g = g.reshape(24, PIVOTS)

    d1 = to_all(g[0:4]).reshape(PIVOTS, PIVOTS)
    g2 = to_all(g[4:12]).reshape(2, PIVOTS, PIVOTS)
    g3 = lax.all_gather(g[12:24], BOTH, axis=1).reshape(3, PIVOTS, PIVOTS)
    w1 = inverse_factor(d1)

    l1 = dot_t(r1, w1)
    l1x = dot(e1, l1)
    l1xx = dot(e2, l1x)
    lp1 = dot_t(g2[1], w1)
    lp1x = dot_t(g3[0], w1)
    q2 = r2 - dot_t(l1x, lp1)
    q2x = dot(e2, q2)
    q3 = r3 - dot_t(l1xx, lp1x)

    rows = jnp.stack([l1, q2, l1xx, q2x, q3]).reshape(5, TR, ROWS, PIVOTS)
    rows = lax.all_to_all(rows.transpose(2, 0, 1, 3), "row", 0, 0, tiled=True)
    rows = lax.all_gather(rows.transpose(1, 2, 0, 3), "col", axis=0)
    rows = rows.transpose(1, 2, 3, 0, 4).reshape(5, TR * TILE, PIVOTS)
    cols = jnp.stack([l1xx, q2x, q3]).reshape(3, TC, COLS, PIVOTS)
    cols = lax.all_to_all(cols.transpose(2, 0, 1, 3), "col", 0, 0, tiled=True)
    cols = lax.all_gather(cols.transpose(1, 2, 0, 3), "row", axis=0)
    cols = cols.transpose(1, 2, 0, 3, 4).reshape(3, TC * TILE, PIVOTS)

    w2 = inverse_factor(g2[0] - dot_t(lp1, lp1))
    lp2 = dot_t(g3[1] - dot_t(lp1x, lp1), w2)
    w3 = inverse_factor(g3[2] - dot_t(lp1x, lp1x) - dot_t(lp2, lp2))

    ka = lax.all_to_all(first.transpose(1, 0, 2, 3), BOTH, 0, 0, tiled=True)
    kf = lax.all_to_all(second.transpose(1, 0, 2, 3), BOTH, 0, 0, tiled=True)
    shape = (ROWS, COLS, TR, TC, TILE)
    back = extended(
        c1, c2, column_masks(c1), column_masks(c2), ka.reshape(shape), kf.reshape(shape)
    )
    back = lax.all_to_all(back.reshape(128, TR, TC, TILE), BOTH, 0, 0, tiled=True)
    assembled = third + back.transpose(1, 0, 2, 3)

    lower_first = rows[0]
    lower_second = dot_t(rows[1], w2)
    l2r = dot_t(rows[3], w2)
    l2c = dot_t(cols[1], w2)
    l3r = dot_t(rows[4] - dot_t(l2r, lp2), w3)
    l3c = dot_t(cols[2] - dot_t(l2c, lp2), w3)
    update = dot_t(rows[2], cols[0]) + dot_t(l2r, l2c) + dot_t(l3r, l3c)
    schur = assembled - update.reshape(TR, TILE, TC, TILE)
    pivot_blocks = PIVOTS // TILE
    row_keep = jnp.arange(TR) * ROWS + lax.axis_index("row") >= pivot_blocks
    col_keep = jnp.arange(TC) * COLS + lax.axis_index("col") >= pivot_blocks
    keep = row_keep[:, None, None, None] & col_keep[None, None, :, None]
    schur = jnp.where(keep, schur, 0.0)
    out = (1, TR, TILE, PIVOTS)
    return (
        lower_first.reshape(out),
        lower_second.reshape(out),
        l3r.reshape(out),
        schur.reshape(1, TR, TILE, 1, TC, TILE),
    )


def solution(mesh):
    front = P("row", None, None, "col", None, None)
    lower = P("row", None, None, None)
    return jax.shard_map(
        per_device,
        mesh=mesh,
        in_specs=(front, front, front, P(), P()),
        out_specs=(lower, lower, lower, front),
        check_vma=False,
    )
```

```python
import jax
import jax.numpy as jnp
from jax import lax
from jax.experimental import pallas as pl
from jax.experimental.pallas import tpu as pltpu
from jax.sharding import PartitionSpec as P

TILE = 128
PIVOTS = 512
BLOCKS = 64
ROWS = 16
COLS = 8
TR = 4
TC = 8
MAXD = 4
F32 = jnp.float32
HI = lax.Precision.HIGHEST
BOTH = ("row", "col")


def full(x):
    return jnp.broadcast_to(x, (8, 128))


def base128(tiles, inv):
    sub = lax.broadcasted_iota(jnp.int32, (8, 128), 0)
    n = len(tiles)
    for b in range(n):
        c0 = 8 * b
        rows = tiles[b]
        cols = [full(rows[:, c0 + c : c0 + c + 1]) for c in range(8)]
        e = [[full(cols[c][r : r + 1, :]) for c in range(r + 1)] for r in range(8)]
        low = [[None] * 8 for _ in range(8)]
        s = [None] * 8
        for j in range(8):
            s[j] = lax.rsqrt(e[j][j])
            for i in range(j + 1, 8):
                low[i][j] = e[i][j] * s[j]
            for i in range(j + 1, 8):
                for k in range(j + 1, i + 1):
                    e[i][k] = e[i][k] - low[i][j] * low[k][j]
        w = [[None] * 8 for _ in range(8)]
        for k in range(8):
            w[k][k] = s[k]
            for i in range(k + 1, 8):
                acc = low[i][k] * w[k][k]
                for m in range(k + 1, i):
                    acc = acc + low[i][m] * w[m][k]
                w[i][k] = -(acc * s[i])
        wcol = []
        for k in range(8):
            v = w[7][k]
            for i in range(6, k - 1, -1):
                v = jnp.where(sub == i, w[i][k], v)
            if k > 0:
                v = jnp.where(sub < k, 0.0, v)
            wcol.append(v)

        def apply(x):
            acc = wcol[0] * full(x[0:1, :])
            for k in range(1, 8):
                acc = acc + wcol[k] * full(x[k : k + 1, :])
            return acc

        upper = apply(rows)
        inv[b] = apply(inv[b])
        if b == n - 1:
            break

        def weighted(x):
            parts = [full(x[i : i + 1, :]) for i in range(8)]
            out = []
            for k in range(8):
                acc = w[k][k] * parts[k]
                for i in range(k + 1, 8):
                    acc = acc + w[i][k] * parts[i]
                out.append(acc)
            return out

        zt = weighted(upper)
        zv = weighted(inv[b])
        for r in range(b + 1, n):
            t = tiles[r]
            v = inv[r]
            for k in range(8):
                c = full(tiles[r][:, c0 + k : c0 + k + 1])
                t = t - c * zt[k]
                v = v - c * zv[k]
            tiles[r] = t
            inv[r] = v
    return inv


def kdot(a, b, dims=(((1,), (0,)), ((), ()))):
    return lax.dot_general(a, b, dims, precision=HI, preferred_element_type=F32)


TN = (((0,), (0,)), ((), ()))


def chol_kernel(d_ref, w_ref, a_ref, wk_ref):
    a_ref[...] = d_ref[...]
    w_ref[...] = jnp.zeros((PIVOTS, PIVOTS), F32)
    ri = lax.broadcasted_iota(jnp.int32, (8, 128), 0)
    ci = lax.broadcasted_iota(jnp.int32, (8, 128), 1)

    def body(kb, carry):
        o = pl.multiple_of(kb * 128, 128)
        tiles = [a_ref[pl.ds(o + 8 * r, 8), pl.ds(o, 128)] for r in range(16)]
        inv = [jnp.where(ri + 8 * r == ci, 1.0, 0.0).astype(F32) for r in range(16)]
        inv = base128(tiles, inv)
        for r in range(16):
            wk_ref[8 * r : 8 * r + 8, :] = inv[r]
        for kk in range(4):

            @pl.when(kb == kk)
            def _(kk=kk):
                k0 = kk * 128
                k1 = k0 + 128
                wk = wk_ref[...]
                if kk > 0:
                    w_ref[k0:k1, :k0] = kdot(wk, w_ref[k0:k1, :k0])
                w_ref[k0:k1, k0:k1] = wk
                if kk < 3:
                    u = kdot(wk, a_ref[k0:k1, k1:])
                    a_ref[k1:, k1:] = a_ref[k1:, k1:] - kdot(u, u, TN)
                    w_ref[k1:, :k1] = w_ref[k1:, :k1] - kdot(u, w_ref[k0:k1, :k1], TN)

        return carry

    lax.fori_loop(0, 4, body, 0)


def inverse_factor(d):
    return pl.pallas_call(
        chol_kernel,
        out_shape=jax.ShapeDtypeStruct((PIVOTS, PIVOTS), F32),
        scratch_shapes=[pltpu.VMEM((PIVOTS, PIVOTS), F32), pltpu.VMEM((128, 128), F32)],
        cost_estimate=pl.CostEstimate(
            flops=25_000_000_000, transcendentals=512, bytes_accessed=2_000_000
        ),
        compiler_params=pltpu.CompilerParams(vmem_limit_bytes=32 << 20),
    )(d)


def panel_kernel(c1_ref, c2_ref, k_ref, r1_ref, r2_ref, r3_ref, g_ref, h_ref, s_ref):
    def row(i, j, t, c):
        return k_ref[i, j, pl.ds(t * 4 + c, 1), :]

    def first(p, carry):
        t = p // ROWS
        i = p % ROWS
        for q in range(4):
            r1_ref[p, q : q + 1, :] = row(i, q, t, 0)
        cp = c1_ref[p]
        cc = jnp.maximum(cp, 0)
        tt = cc // ROWS
        ii = cc % ROWS
        for q in range(8):
            cq = c1_ref[q]
            qq = jnp.maximum(cq, 0)
            got = row(ii, qq % COLS, tt, qq // COLS)
            got = jnp.where((cp >= 0) & (cq >= 0), got, 0.0)
            val = row(i, q, t, 2) + got
            s_ref[p, q : q + 1, :] = val
            if q < 4:
                r2_ref[p, q : q + 1, :] = val
        return carry

    lax.fori_loop(0, BLOCKS, first, 0)

    def second(p, carry):
        t = p // ROWS
        i = p % ROWS
        cp = c2_ref[p]
        cc = jnp.maximum(cp, 0)
        for q in range(4):
            cq = c2_ref[q]
            qq = jnp.maximum(cq, 0)
            got = s_ref[cc, pl.ds(qq, 1), :]
            got = jnp.where((cp >= 0) & (cq >= 0), got, 0.0)
            r3_ref[p, q : q + 1, :] = row(i, q, t, 3) + got
        c12 = c1_ref[cc]
        j = p % COLS
        s = p // COLS
        h_ref[j, 0, s] = jnp.where(
            (cp >= 0) & (c12 >= 0), r1_ref[jnp.maximum(c12, 0)], 0.0
        )
        h_ref[j, 1, s] = jnp.where(cp >= 0, r2_ref[cc], 0.0)
        h_ref[j, 2, s] = r3_ref[p]
        return carry

    lax.fori_loop(0, BLOCKS, second, 0)
    g_ref[0:4] = r1_ref[0:4]
    g_ref[4:8] = r2_ref[0:4]
    g_ref[20:24] = r3_ref[0:4]
    for q in range(4):
        a = c1_ref[q]
        g_ref[8 + q] = jnp.where(a >= 0, r1_ref[jnp.maximum(a, 0)], 0.0)
        b = c2_ref[q]
        c = c1_ref[jnp.maximum(b, 0)]
        g_ref[12 + q] = jnp.where((b >= 0) & (c >= 0), r1_ref[jnp.maximum(c, 0)], 0.0)
        g_ref[16 + q] = jnp.where(b >= 0, r2_ref[jnp.maximum(b, 0)], 0.0)


def panels(c1, c2, k):
    smem = pl.BlockSpec(memory_space=pltpu.SMEM)
    vmem = pl.BlockSpec(memory_space=pltpu.VMEM)
    return pl.pallas_call(
        panel_kernel,
        out_shape=[jax.ShapeDtypeStruct((BLOCKS, 4, 128), F32)] * 3
        + [
            jax.ShapeDtypeStruct((24, 4, 128), F32),
            jax.ShapeDtypeStruct((COLS, 3, TC, 4, 128), F32),
        ],
        in_specs=[smem, smem, vmem],
        out_specs=[vmem] * 5,
        scratch_shapes=[pltpu.VMEM((BLOCKS, 8, 128), F32)],
        compiler_params=pltpu.CompilerParams(vmem_limit_bytes=32 << 20),
    )(c1, c2, k)


def extend_kernel(c1_ref, c2_ref, m1_ref, m2_ref, a_ref, o_ref, s_ref):
    def moved(src, m_ref, c):
        cc = jnp.maximum(c, 0)
        t = cc // ROWS
        i = cc % ROWS
        x = [src[i, j, t] for j in range(COLS)]
        x = x + [pltpu.roll(x[j], 7, 0) for j in range(MAXD)]
        out = []
        for j in range(COLS):
            acc = m_ref[0, j] * x[j]
            for d in range(1, MAXD + 1):
                acc = acc + m_ref[d, j] * x[j + d]
            out.append(jnp.where(c >= 0, acc, 0.0))
        return out

    def first(p, carry):
        got = moved(a_ref, m1_ref, c1_ref[p])
        t = p // ROWS
        i = p % ROWS
        for j in range(COLS):
            s_ref[i, j, t] = a_ref[i, j, TR + t] + got[j]
        return carry

    lax.fori_loop(0, BLOCKS, first, 0)

    def second(p, carry):
        got = moved(s_ref, m2_ref, c2_ref[p])
        t = p // ROWS
        i = p % ROWS
        for j in range(COLS):
            o_ref[i, j, t] = got[j]
        return carry

    lax.fori_loop(0, BLOCKS, second, 0)


def extended(c1, c2, m1, m2, a):
    smem = pl.BlockSpec(memory_space=pltpu.SMEM)
    vmem = pl.BlockSpec(memory_space=pltpu.VMEM)
    shape = (ROWS, COLS, TR, TC, 128)
    return pl.pallas_call(
        extend_kernel,
        out_shape=jax.ShapeDtypeStruct(shape, F32),
        in_specs=[smem, smem, vmem, vmem, vmem],
        out_specs=vmem,
        scratch_shapes=[pltpu.VMEM(shape, F32)],
        compiler_params=pltpu.CompilerParams(vmem_limit_bytes=32 << 20),
    )(c1, c2, m1, m2, a)


def dot(a, b):
    return jnp.dot(a, b, precision=HI, preferred_element_type=F32)


def dot_t(a, b):
    return lax.dot_general(
        a, b, (((1,), (1,)), ((), ())), precision=HI, preferred_element_type=F32
    )


def child_of(block_map):
    blocks = jnp.arange(BLOCKS, dtype=jnp.int32)
    hit = block_map[None, :] == blocks[:, None]
    ids = jnp.arange(block_map.shape[0], dtype=jnp.int32) + (PIVOTS // TILE + 1)
    return jnp.sum(jnp.where(hit, ids[None, :], 0), axis=1) - 1


def column_masks(child):
    blocks = jnp.arange(BLOCKS, dtype=jnp.int32)
    hits = jnp.stack([child == blocks + d for d in range(MAXD + 1)])
    hits = hits.reshape(MAXD + 1, TC, COLS).transpose(0, 2, 1).astype(F32)
    return jnp.broadcast_to(hits[..., None], (MAXD + 1, COLS, TC, 128))


def one_hot(child):
    return (child[:, None] == jnp.arange(BLOCKS, dtype=jnp.int32)[None, :]).astype(F32)


def to_all(rows):
    n = rows.shape[0]
    many = jnp.broadcast_to(rows[None], (128, n, PIVOTS))
    return lax.all_to_all(many, BOTH, 0, 0, tiled=True).transpose(1, 0, 2)


def after(x, y):
    return lax.optimization_barrier((x, y))


def per_device(front_first, front_second, front_third, map_second, map_third):
    first = front_first.reshape(TR, TILE, TC, TILE)
    second = front_second.reshape(TR, TILE, TC, TILE)
    third = front_third.reshape(TR, TILE, TC, TILE)
    c1 = child_of(map_second)
    c2 = child_of(map_third)
    e1 = one_hot(c1)
    e2 = one_hot(c2)

    packed = jnp.concatenate([first[:, :, 0:2], second[:, :, 0:1], third[:, :, 0:1]], axis=2)
    packed = packed.transpose(1, 0, 2, 3).reshape(128, 16, 128)
    packed = lax.all_to_all(packed, BOTH, 0, 0, tiled=True).reshape(ROWS, COLS, 16, 128)
    r1, r2, r3, g, h = panels(c1, c2, packed)
    r1, r2, r3 = (r.reshape(BLOCKS, PIVOTS) for r in (r1, r2, r3))
    g = g.reshape(24, PIVOTS)

    g3 = lax.all_gather(g[12:24], BOTH, axis=1).reshape(3, PIVOTS, PIVOTS)
    d1 = to_all(g[0:4]).reshape(PIVOTS, PIVOTS)
    g_next, d1 = after(g[4:12], d1)
    g2 = to_all(g_next).reshape(2, PIVOTS, PIVOTS)
    w1 = inverse_factor(d1)

    (h, w1), g2 = after((h, w1), g2)
    cols = lax.all_to_all(h.reshape(COLS, 3, TC, PIVOTS), "col", 0, 0, tiled=True)
    cols = lax.all_gather(cols.transpose(1, 2, 0, 3), "row", axis=0)

    lp1 = dot_t(g2[1], w1)
    d2 = g2[0] - dot_t(lp1, lp1)
    (first, second), d2 = after((first, second), d2)
    moving = jnp.concatenate([first.transpose(1, 0, 2, 3), second.transpose(1, 0, 2, 3)], axis=1)
    moving = lax.all_to_all(moving, BOTH, 0, 0, tiled=True)
    w2 = inverse_factor(d2)

    lp1x = dot_t(g3[0], w1)
    lp2 = dot_t(g3[1] - dot_t(lp1x, lp1), w2)
    w3 = inverse_factor(g3[2] - dot_t(lp1x, lp1x) - dot_t(lp2, lp2))

    l1 = dot_t(r1, w1)
    l1x = dot(e1, l1)
    l1xx = dot(e2, l1x)
    l2 = dot_t(r2 - dot_t(l1x, lp1), w2)
    l2x = dot(e2, l2)
    l3 = dot_t(r3 - dot_t(l1xx, lp1x) - dot_t(l2x, lp2), w3)
    rows = jnp.stack([l1, l2, l1xx, l2x, l3]).reshape(5, TR, ROWS, PIVOTS)
    rows, moving = after(rows, moving)
    rows = lax.all_to_all(rows.transpose(2, 0, 1, 3), "row", 0, 0, tiled=True)
    rows = lax.all_gather(rows.transpose(1, 2, 0, 3), "col", axis=0)
    rows = rows.transpose(1, 2, 3, 0, 4).reshape(5, TR * TILE, PIVOTS)

    back = extended(
        c1,
        c2,
        column_masks(c1),
        column_masks(c2),
        moving.reshape(ROWS, COLS, 2 * TR, TC, TILE),
    )
    back = lax.all_to_all(back.reshape(128, TR, TC, TILE), BOTH, 0, 0, tiled=True)
    assembled = third + back.transpose(1, 0, 2, 3)

    cols = cols.transpose(1, 2, 0, 3, 4).reshape(3, TC * TILE, PIVOTS)
    l1c = dot_t(cols[0], w1)
    l2c = dot_t(cols[1] - dot_t(l1c, lp1), w2)
    l3c = dot_t(cols[2] - dot_t(l1c, lp1x) - dot_t(l2c, lp2), w3)
    lower_first = rows[0]
    lower_second = rows[1]
    l3r = rows[4]
    update = dot_t(rows[2], l1c) + dot_t(rows[3], l2c) + dot_t(l3r, l3c)
    schur = assembled - update.reshape(TR, TILE, TC, TILE)
    pivot_blocks = PIVOTS // TILE
    row_keep = jnp.arange(TR) * ROWS + lax.axis_index("row") >= pivot_blocks
    col_keep = jnp.arange(TC) * COLS + lax.axis_index("col") >= pivot_blocks
    keep = row_keep[:, None, None, None] & col_keep[None, None, :, None]
    schur = jnp.where(keep, schur, 0.0)
    out = (1, TR, TILE, PIVOTS)
    return (
        lower_first.reshape(out),
        lower_second.reshape(out),
        l3r.reshape(out),
        schur.reshape(1, TR, TILE, 1, TC, TILE),
    )


def solution(mesh):
    front = P("row", None, None, "col", None, None)
    lower = P("row", None, None, None)
    return jax.shard_map(
        per_device,
        mesh=mesh,
        in_specs=(front, front, front, P(), P()),
        out_specs=(lower, lower, lower, front),
        check_vma=False,
    )
```

```python
import jax
import jax.numpy as jnp
from jax import lax
from jax.experimental import pallas as pl
from jax.experimental.pallas import tpu as pltpu
from jax.sharding import PartitionSpec as P

TILE = 128
PIVOTS = 512
BLOCKS = 64
ROWS = 16
COLS = 8
TR = 4
TC = 8
MAXD = 4
F32 = jnp.float32
HI = lax.Precision.HIGHEST
BOTH = ("row", "col")


def full(x):
    return jnp.broadcast_to(x, (8, 128))


def base128(tiles, inv):
    sub = lax.broadcasted_iota(jnp.int32, (8, 128), 0)
    n = len(tiles)
    for b in range(n):
        c0 = 8 * b
        rows = tiles[b]
        cols = [full(rows[:, c0 + c : c0 + c + 1]) for c in range(8)]
        e = [[full(cols[c][r : r + 1, :]) for c in range(r + 1)] for r in range(8)]
        low = [[None] * 8 for _ in range(8)]
        s = [None] * 8
        for j in range(8):
            s[j] = lax.rsqrt(e[j][j])
            for i in range(j + 1, 8):
                low[i][j] = e[i][j] * s[j]
            for i in range(j + 1, 8):
                for k in range(j + 1, i + 1):
                    e[i][k] = e[i][k] - low[i][j] * low[k][j]
        w = [[None] * 8 for _ in range(8)]
        for k in range(8):
            w[k][k] = s[k]
            for i in range(k + 1, 8):
                acc = low[i][k] * w[k][k]
                for m in range(k + 1, i):
                    acc = acc + low[i][m] * w[m][k]
                w[i][k] = -(acc * s[i])
        wcol = []
        for k in range(8):
            v = w[7][k]
            for i in range(6, k - 1, -1):
                v = jnp.where(sub == i, w[i][k], v)
            if k > 0:
                v = jnp.where(sub < k, 0.0, v)
            wcol.append(v)

        def apply(x):
            acc = wcol[0] * full(x[0:1, :])
            for k in range(1, 8):
                acc = acc + wcol[k] * full(x[k : k + 1, :])
            return acc

        upper = apply(rows)
        inv[b] = apply(inv[b])
        if b == n - 1:
            break

        def weighted(x):
            parts = [full(x[i : i + 1, :]) for i in range(8)]
            out = []
            for k in range(8):
                acc = w[k][k] * parts[k]
                for i in range(k + 1, 8):
                    acc = acc + w[i][k] * parts[i]
                out.append(acc)
            return out

        zt = weighted(upper)
        zv = weighted(inv[b])
        for r in range(b + 1, n):
            t = tiles[r]
            v = inv[r]
            for k in range(8):
                c = full(tiles[r][:, c0 + k : c0 + k + 1])
                t = t - c * zt[k]
                v = v - c * zv[k]
            tiles[r] = t
            inv[r] = v
    return inv


def kdot(a, b, dims=(((1,), (0,)), ((), ()))):
    return lax.dot_general(a, b, dims, precision=HI, preferred_element_type=F32)


TN = (((0,), (0,)), ((), ()))


def chol_kernel(d_ref, w_ref, a_ref, wk_ref):
    a_ref[...] = d_ref[...]
    w_ref[...] = jnp.zeros((PIVOTS, PIVOTS), F32)
    ri = lax.broadcasted_iota(jnp.int32, (8, 128), 0)
    ci = lax.broadcasted_iota(jnp.int32, (8, 128), 1)

    def body(kb, carry):
        o = pl.multiple_of(kb * 128, 128)
        tiles = [a_ref[pl.ds(o + 8 * r, 8), pl.ds(o, 128)] for r in range(16)]
        inv = [jnp.where(ri + 8 * r == ci, 1.0, 0.0).astype(F32) for r in range(16)]
        inv = base128(tiles, inv)
        for r in range(16):
            wk_ref[8 * r : 8 * r + 8, :] = inv[r]
        for kk in range(4):

            @pl.when(kb == kk)
            def _(kk=kk):
                k0 = kk * 128
                k1 = k0 + 128
                wk = wk_ref[...]
                if kk > 0:
                    w_ref[k0:k1, :k0] = kdot(wk, w_ref[k0:k1, :k0])
                w_ref[k0:k1, k0:k1] = wk
                if kk < 3:
                    u = kdot(wk, a_ref[k0:k1, k1:])
                    a_ref[k1:, k1:] = a_ref[k1:, k1:] - kdot(u, u, TN)
                    w_ref[k1:, :k1] = w_ref[k1:, :k1] - kdot(u, w_ref[k0:k1, :k1], TN)

        return carry

    lax.fori_loop(0, 4, body, 0)


def inverse_factor(d):
    return pl.pallas_call(
        chol_kernel,
        out_shape=jax.ShapeDtypeStruct((PIVOTS, PIVOTS), F32),
        scratch_shapes=[pltpu.VMEM((PIVOTS, PIVOTS), F32), pltpu.VMEM((128, 128), F32)],
        cost_estimate=pl.CostEstimate(
            flops=25_000_000_000, transcendentals=512, bytes_accessed=2_000_000
        ),
        compiler_params=pltpu.CompilerParams(vmem_limit_bytes=32 << 20),
    )(d)


SMEM = pl.BlockSpec(memory_space=pltpu.SMEM)
VMEM = pl.BlockSpec(memory_space=pltpu.VMEM)


def assemble(c1_ref, c2_ref, k_ref, r1_ref, r2_ref, r3_ref, s_ref, n1, n2, n3):
    def row(i, j, t, c):
        return k_ref[i, j, pl.ds(t * 4 + c, 1), :]

    def load(p, carry):
        t = p // ROWS
        i = p % ROWS
        for q in range(4):
            r1_ref[p, q : q + 1, :] = row(i, q, t, 0)
        return carry

    lax.fori_loop(0, n1, load, 0)

    def first(p, carry):
        t = p // ROWS
        i = p % ROWS
        cp = c1_ref[p]
        cc = jnp.maximum(cp, 0)
        tt = cc // ROWS
        ii = cc % ROWS
        for q in range(8):
            cq = c1_ref[q]
            qq = jnp.maximum(cq, 0)
            got = row(ii, qq % COLS, tt, qq // COLS)
            got = jnp.where((cp >= 0) & (cq >= 0), got, 0.0)
            val = row(i, q, t, 2) + got
            s_ref[p, q : q + 1, :] = val
            if q < 4:
                r2_ref[p, q : q + 1, :] = val
        return carry

    lax.fori_loop(0, n2, first, 0)

    def second(p, carry):
        t = p // ROWS
        i = p % ROWS
        cp = c2_ref[p]
        cc = jnp.maximum(cp, 0)
        for q in range(4):
            cq = c2_ref[q]
            qq = jnp.maximum(cq, 0)
            got = s_ref[cc, pl.ds(qq, 1), :]
            got = jnp.where((cp >= 0) & (cq >= 0), got, 0.0)
            r3_ref[p, q : q + 1, :] = row(i, q, t, 3) + got
        return carry

    lax.fori_loop(0, n3, second, 0)


def panel_kernel(c1_ref, c2_ref, k_ref, r1_ref, r2_ref, r3_ref, h_ref, s_ref):
    assemble(
        c1_ref, c2_ref, k_ref, r1_ref, r2_ref, r3_ref, s_ref, BLOCKS, BLOCKS, BLOCKS
    )

    def column_side(p, carry):
        cp = c2_ref[p]
        cc = jnp.maximum(cp, 0)
        c12 = c1_ref[cc]
        j = p % COLS
        s = p // COLS
        h_ref[j, 0, s] = jnp.where(
            (cp >= 0) & (c12 >= 0), r1_ref[jnp.maximum(c12, 0)], 0.0
        )
        h_ref[j, 1, s] = jnp.where(cp >= 0, r2_ref[cc], 0.0)
        h_ref[j, 2, s] = r3_ref[p]
        return carry

    lax.fori_loop(0, BLOCKS, column_side, 0)


def pivot_kernel(c1_ref, c2_ref, k_ref, g_ref, r1_ref, r2_ref, r3_ref, s_ref):
    assemble(c1_ref, c2_ref, k_ref, r1_ref, r2_ref, r3_ref, s_ref, 12, 8, 4)
    g_ref[0:4] = r1_ref[0:4]
    g_ref[4:8] = r2_ref[0:4]
    g_ref[20:24] = r3_ref[0:4]
    for q in range(4):
        a = c1_ref[q]
        g_ref[8 + q] = jnp.where(a >= 0, r1_ref[jnp.maximum(a, 0)], 0.0)
        b = c2_ref[q]
        c = c1_ref[jnp.maximum(b, 0)]
        g_ref[12 + q] = jnp.where((b >= 0) & (c >= 0), r1_ref[jnp.maximum(c, 0)], 0.0)
        g_ref[16 + q] = jnp.where(b >= 0, r2_ref[jnp.maximum(b, 0)], 0.0)


def panels(c1, c2, k):
    return pl.pallas_call(
        panel_kernel,
        out_shape=[jax.ShapeDtypeStruct((BLOCKS, 4, 128), F32)] * 3
        + [jax.ShapeDtypeStruct((COLS, 3, TC, 4, 128), F32)],
        in_specs=[SMEM, SMEM, VMEM],
        out_specs=[VMEM] * 4,
        scratch_shapes=[pltpu.VMEM((BLOCKS, 8, 128), F32)],
        compiler_params=pltpu.CompilerParams(vmem_limit_bytes=32 << 20),
    )(c1, c2, k)


def pivots(c1, c2, k):
    return pl.pallas_call(
        pivot_kernel,
        out_shape=jax.ShapeDtypeStruct((24, 4, 128), F32),
        in_specs=[SMEM, SMEM, VMEM],
        out_specs=VMEM,
        scratch_shapes=[pltpu.VMEM((12, 4, 128), F32)]
        + [pltpu.VMEM((8, 4, 128), F32)] * 2
        + [pltpu.VMEM((8, 8, 128), F32)],
        compiler_params=pltpu.CompilerParams(vmem_limit_bytes=32 << 20),
    )(c1, c2, k)


def pack_kernel(a_ref, b_ref, o_ref):
    o_ref[:, 0, 0] = a_ref[0]
    o_ref[:, 1, 0] = b_ref[0]


def pack(a, b):
    block = pl.BlockSpec((1, TILE, TC, TILE), lambda t: (t, 0, 0, 0))
    return pl.pallas_call(
        pack_kernel,
        grid=(TR,),
        out_shape=jax.ShapeDtypeStruct((TILE, 2, TR, TC, TILE), F32),
        in_specs=[block, block],
        out_specs=pl.BlockSpec((TILE, 2, 1, TC, TILE), lambda t: (0, 0, t, 0, 0)),
        compiler_params=pltpu.CompilerParams(vmem_limit_bytes=32 << 20),
    )(a, b)


def extend_kernel(c1_ref, c2_ref, m1_ref, m2_ref, a_ref, o_ref, s_ref):
    def moved(src, m_ref, c):
        cc = jnp.maximum(c, 0)
        t = cc // ROWS
        i = cc % ROWS
        x = [src[i, j, t] for j in range(COLS)]
        x = x + [pltpu.roll(x[j], 7, 0) for j in range(MAXD)]
        out = []
        for j in range(COLS):
            acc = m_ref[0, j] * x[j]
            for d in range(1, MAXD + 1):
                acc = acc + m_ref[d, j] * x[j + d]
            out.append(jnp.where(c >= 0, acc, 0.0))
        return out

    def first(p, carry):
        got = moved(a_ref, m1_ref, c1_ref[p])
        t = p // ROWS
        i = p % ROWS
        for j in range(COLS):
            s_ref[i, j, t] = a_ref[i, j, TR + t] + got[j]
        return carry

    lax.fori_loop(0, BLOCKS, first, 0)

    def second(p, carry):
        got = moved(s_ref, m2_ref, c2_ref[p])
        t = p // ROWS
        i = p % ROWS
        for j in range(COLS):
            o_ref[i, j, t] = got[j]
        return carry

    lax.fori_loop(0, BLOCKS, second, 0)


def extended(c1, c2, m1, m2, a):
    smem = pl.BlockSpec(memory_space=pltpu.SMEM)
    vmem = pl.BlockSpec(memory_space=pltpu.VMEM)
    shape = (ROWS, COLS, TR, TC, 128)
    return pl.pallas_call(
        extend_kernel,
        out_shape=jax.ShapeDtypeStruct(shape, F32),
        in_specs=[smem, smem, vmem, vmem, vmem],
        out_specs=vmem,
        scratch_shapes=[pltpu.VMEM(shape, F32)],
        compiler_params=pltpu.CompilerParams(vmem_limit_bytes=32 << 20),
    )(c1, c2, m1, m2, a)


def dot(a, b):
    return jnp.dot(a, b, precision=HI, preferred_element_type=F32)


def dot_t(a, b, precision=HI):
    return lax.dot_general(
        a, b, (((1,), (1,)), ((), ())), precision=precision, preferred_element_type=F32
    )


def child_of(block_map):
    blocks = jnp.arange(BLOCKS, dtype=jnp.int32)
    hit = block_map[None, :] == blocks[:, None]
    ids = jnp.arange(block_map.shape[0], dtype=jnp.int32) + (PIVOTS // TILE + 1)
    return jnp.sum(jnp.where(hit, ids[None, :], 0), axis=1) - 1


def column_masks(child):
    blocks = jnp.arange(BLOCKS, dtype=jnp.int32)
    hits = jnp.stack([child == blocks + d for d in range(MAXD + 1)])
    hits = hits.reshape(MAXD + 1, TC, COLS).transpose(0, 2, 1).astype(F32)
    return jnp.broadcast_to(hits[..., None], (MAXD + 1, COLS, TC, 128))


def one_hot(child):
    return (child[:, None] == jnp.arange(BLOCKS, dtype=jnp.int32)[None, :]).astype(F32)


def own_rows(rows, later):
    n = rows.shape[0]
    half = PIVOTS // 2
    many = rows.reshape(n, TR, ROWS, 2, half).transpose(2, 3, 0, 1, 4)
    many = jnp.broadcast_to(many[:, None], (ROWS, COLS // 2, 2, n, TR, half))
    mine = lax.all_to_all(
        many.reshape(ROWS * COLS, n, TR, half), BOTH, 0, 0, tiled=True
    )
    mine, later = after(mine, later)
    other = lax.ppermute(mine, "col", [(j, j ^ 1) for j in range(COLS)])
    even = lax.axis_index("col") % 2 == 0
    halves = [jnp.where(even, mine, other), jnp.where(even, other, mine)]
    return jnp.concatenate(halves, axis=3).transpose(1, 2, 0, 3), later


def after(x, y):
    return lax.optimization_barrier((x, y))


def per_device(front_first, front_second, front_third, map_second, map_third):
    first = front_first.reshape(TR, TILE, TC, TILE)
    second = front_second.reshape(TR, TILE, TC, TILE)
    third = front_third.reshape(TR, TILE, TC, TILE)
    c1 = child_of(map_second)
    c2 = child_of(map_third)
    e1 = one_hot(c1)
    e2 = one_hot(c2)

    packed = jnp.concatenate([first[:, :, 0:2], second[:, :, 0:1], third[:, :, 0:1]], axis=2)
    packed = packed.transpose(1, 0, 2, 3)

    top = lax.all_to_all(packed[:, 0], BOTH, 0, 0, tiled=True)
    g = pivots(c1, c2, top.reshape(ROWS, COLS, 4, 128)).reshape(24, PIVOTS)
    packed, g = after(packed, g)
    pivot = lax.all_gather(g, BOTH, axis=1).reshape(6, PIVOTS, PIVOTS)

    packed = lax.all_to_all(packed.reshape(128, 16, 128), BOTH, 0, 0, tiled=True)
    r1, r2, r3, h = panels(c1, c2, packed.reshape(ROWS, COLS, 16, 128))
    r1, r2, r3 = (r.reshape(BLOCKS, PIVOTS) for r in (r1, r2, r3))
    cols = lax.all_to_all(h.reshape(COLS, 3, TC, PIVOTS), "col", 0, 0, tiled=True)
    cols = cols.transpose(1, 2, 0, 3)
    (first, second), cols = after((first, second), cols)
    moving = pack(first, second).reshape(TILE, 2 * TR, TC, TILE)
    (moving, cols), pivot = after((moving, cols), pivot)
    cols = lax.all_gather(cols, "row", axis=0)
    moving = lax.all_to_all(moving, BOTH, 0, 0, tiled=True)

    w1 = inverse_factor(pivot[0])
    lp1 = dot_t(pivot[2], w1)
    w2 = inverse_factor(pivot[1] - dot_t(lp1, lp1))
    lp1x = dot_t(pivot[3], w1)
    lp2 = dot_t(pivot[4] - dot_t(lp1x, lp1), w2)
    d3 = pivot[5] - dot_t(lp1x, lp1x) - dot_t(lp2, lp2)


    (moving, r1, r2, r3), w2 = after((moving, r1, r2, r3), w2)
    back = extended(
        c1,
        c2,
        column_masks(c1),
        column_masks(c2),
        moving.reshape(ROWS, COLS, 2 * TR, TC, TILE),
    )
    back, d3 = after(back, d3)
    back = lax.all_to_all(back.reshape(128, TR, TC, TILE), BOTH, 0, 0, tiled=True)
    w3 = inverse_factor(d3)

    l1 = dot_t(r1, w1)
    l1x = dot(e1, l1)
    l1xx = dot(e2, l1x)
    l2 = dot_t(r2 - dot_t(l1x, lp1), w2)
    l2x = dot(e2, l2)
    l3 = dot_t(r3 - dot_t(l1xx, lp1x) - dot_t(l2x, lp2), w3)
    (l1, l2, l3, cols), back = after((l1, l2, l3, cols), back)
    cols = cols.transpose(1, 2, 0, 3, 4).reshape(3, TC * TILE, PIVOTS)
    high = lax.Precision.HIGH
    l1c = dot_t(cols[0], w1, high)
    l2c = dot_t(cols[1] - dot_t(l1c, lp1, high), w2, high)
    l3c = cols[2] - dot_t(l1c, lp1x, high) - dot_t(l2c, lp2, high)
    l3c = dot_t(l3c, w3, high)
    rows, (l1, l2, l1c, l2c, l3c) = own_rows(
        jnp.stack([l1xx, l2x, l3]), (l1, l2, l1c, l2c, l3c)
    )
    rows = rows.reshape(3, TR * TILE, PIVOTS)
    l3r = rows[2]
    update = (
        dot_t(rows[0], l1c, high)
        + dot_t(rows[1], l2c, high)
        + dot_t(l3r, l3c, high)
    )
    outer, update = own_rows(jnp.stack([l1, l2]), update)
    lower_first, lower_second = outer[0], outer[1]
    assembled = third + back.transpose(1, 0, 2, 3)

    schur = assembled - update.reshape(TR, TILE, TC, TILE)
    pivot_blocks = PIVOTS // TILE
    row_keep = jnp.arange(TR) * ROWS + lax.axis_index("row") >= pivot_blocks
    col_keep = jnp.arange(TC) * COLS + lax.axis_index("col") >= pivot_blocks
    keep = row_keep[:, None, None, None] & col_keep[None, None, :, None]
    schur = jnp.where(keep, schur, 0.0)
    out = (1, TR, TILE, PIVOTS)
    return (
        lower_first.reshape(out),
        lower_second.reshape(out),
        l3r.reshape(out),
        schur.reshape(1, TR, TILE, 1, TC, TILE),
    )


def solution(mesh):
    front = P("row", None, None, "col", None, None)
    lower = P("row", None, None, None)
    return jax.shard_map(
        per_device,
        mesh=mesh,
        in_specs=(front, front, front, P(), P()),
        out_specs=(lower, lower, lower, front),
        check_vma=False,
    )
```

```python
import jax
import jax.numpy as jnp
from jax import lax
from jax.experimental import pallas as pl
from jax.experimental.pallas import tpu as pltpu
from jax.sharding import PartitionSpec as P

TILE = 128
PIVOTS = 512
BLOCKS = 64
ROWS = 16
COLS = 8
TR = 4
TC = 8
MAXD = 4
F32 = jnp.float32
HI = lax.Precision.HIGHEST
BOTH = ("row", "col")


def full(x):
    return jnp.broadcast_to(x, (8, 128))


def base128(tiles, inv):
    sub = lax.broadcasted_iota(jnp.int32, (8, 128), 0)
    n = len(tiles)
    for b in range(n):
        c0 = 8 * b
        rows = tiles[b]
        cols = [full(rows[:, c0 + c : c0 + c + 1]) for c in range(8)]
        e = [[full(cols[c][r : r + 1, :]) for c in range(r + 1)] for r in range(8)]
        low = [[None] * 8 for _ in range(8)]
        s = [None] * 8
        for j in range(8):
            s[j] = lax.rsqrt(e[j][j])
            for i in range(j + 1, 8):
                low[i][j] = e[i][j] * s[j]
            for i in range(j + 1, 8):
                for k in range(j + 1, i + 1):
                    e[i][k] = e[i][k] - low[i][j] * low[k][j]
        w = [[None] * 8 for _ in range(8)]
        for k in range(8):
            w[k][k] = s[k]
            for i in range(k + 1, 8):
                acc = low[i][k] * w[k][k]
                for m in range(k + 1, i):
                    acc = acc + low[i][m] * w[m][k]
                w[i][k] = -(acc * s[i])
        wcol = []
        for k in range(8):
            v = w[7][k]
            for i in range(6, k - 1, -1):
                v = jnp.where(sub == i, w[i][k], v)
            if k > 0:
                v = jnp.where(sub < k, 0.0, v)
            wcol.append(v)

        def apply(x):
            acc = wcol[0] * full(x[0:1, :])
            for k in range(1, 8):
                acc = acc + wcol[k] * full(x[k : k + 1, :])
            return acc

        upper = apply(rows)
        inv[b] = apply(inv[b])
        if b == n - 1:
            break

        def weighted(x):
            parts = [full(x[i : i + 1, :]) for i in range(8)]
            out = []
            for k in range(8):
                acc = w[k][k] * parts[k]
                for i in range(k + 1, 8):
                    acc = acc + w[i][k] * parts[i]
                out.append(acc)
            return out

        zt = weighted(upper)
        zv = weighted(inv[b])
        for r in range(b + 1, n):
            t = tiles[r]
            v = inv[r]
            for k in range(8):
                c = full(tiles[r][:, c0 + k : c0 + k + 1])
                t = t - c * zt[k]
                v = v - c * zv[k]
            tiles[r] = t
            inv[r] = v
    return inv


def kdot(a, b, dims=(((1,), (0,)), ((), ()))):
    return lax.dot_general(a, b, dims, precision=HI, preferred_element_type=F32)


TN = (((0,), (0,)), ((), ()))


def chol_kernel(d_ref, w_ref, a_ref, wk_ref):
    a_ref[...] = d_ref[...]
    w_ref[...] = jnp.zeros((PIVOTS, PIVOTS), F32)
    ri = lax.broadcasted_iota(jnp.int32, (8, 128), 0)
    ci = lax.broadcasted_iota(jnp.int32, (8, 128), 1)

    def body(kb, carry):
        o = pl.multiple_of(kb * 128, 128)
        tiles = [a_ref[pl.ds(o + 8 * r, 8), pl.ds(o, 128)] for r in range(16)]
        inv = [jnp.where(ri + 8 * r == ci, 1.0, 0.0).astype(F32) for r in range(16)]
        inv = base128(tiles, inv)
        for r in range(16):
            wk_ref[8 * r : 8 * r + 8, :] = inv[r]
        for kk in range(4):

            @pl.when(kb == kk)
            def _(kk=kk):
                k0 = kk * 128
                k1 = k0 + 128
                wk = wk_ref[...]
                if kk > 0:
                    w_ref[k0:k1, :k0] = kdot(wk, w_ref[k0:k1, :k0])
                w_ref[k0:k1, k0:k1] = wk
                if kk < 3:
                    u = kdot(wk, a_ref[k0:k1, k1:])
                    a_ref[k1:, k1:] = a_ref[k1:, k1:] - kdot(u, u, TN)
                    w_ref[k1:, :k1] = w_ref[k1:, :k1] - kdot(u, w_ref[k0:k1, :k1], TN)

        return carry

    lax.fori_loop(0, 4, body, 0)


def inverse_factor(d):
    return pl.pallas_call(
        chol_kernel,
        out_shape=jax.ShapeDtypeStruct((PIVOTS, PIVOTS), F32),
        scratch_shapes=[pltpu.VMEM((PIVOTS, PIVOTS), F32), pltpu.VMEM((128, 128), F32)],
        cost_estimate=pl.CostEstimate(
            flops=25_000_000_000, transcendentals=512, bytes_accessed=2_000_000
        ),
        compiler_params=pltpu.CompilerParams(vmem_limit_bytes=32 << 20),
    )(d)


SMEM = pl.BlockSpec(memory_space=pltpu.SMEM)
VMEM = pl.BlockSpec(memory_space=pltpu.VMEM)


def assemble(c1_ref, c2_ref, k_ref, r1_ref, r2_ref, r3_ref, s_ref, n1, n2, n3):
    def row(i, j, t, c):
        return k_ref[i, j, pl.ds(t * 4 + c, 1), :]

    def load(p, carry):
        t = p // ROWS
        i = p % ROWS
        for q in range(4):
            r1_ref[p, q : q + 1, :] = row(i, q, t, 0)
        return carry

    lax.fori_loop(0, n1, load, 0)

    def first(p, carry):
        t = p // ROWS
        i = p % ROWS
        cp = c1_ref[p]
        cc = jnp.maximum(cp, 0)
        tt = cc // ROWS
        ii = cc % ROWS
        for q in range(8):
            cq = c1_ref[q]
            qq = jnp.maximum(cq, 0)
            got = row(ii, qq % COLS, tt, qq // COLS)
            got = jnp.where((cp >= 0) & (cq >= 0), got, 0.0)
            val = row(i, q, t, 2) + got
            s_ref[p, q : q + 1, :] = val
            if q < 4:
                r2_ref[p, q : q + 1, :] = val
        return carry

    lax.fori_loop(0, n2, first, 0)

    def second(p, carry):
        t = p // ROWS
        i = p % ROWS
        cp = c2_ref[p]
        cc = jnp.maximum(cp, 0)
        for q in range(4):
            cq = c2_ref[q]
            qq = jnp.maximum(cq, 0)
            got = s_ref[cc, pl.ds(qq, 1), :]
            got = jnp.where((cp >= 0) & (cq >= 0), got, 0.0)
            r3_ref[p, q : q + 1, :] = row(i, q, t, 3) + got
        return carry

    lax.fori_loop(0, n3, second, 0)


def panel_kernel(c1_ref, c2_ref, k_ref, r1_ref, r2_ref, r3_ref, h_ref, s_ref):
    assemble(
        c1_ref, c2_ref, k_ref, r1_ref, r2_ref, r3_ref, s_ref, BLOCKS, BLOCKS, BLOCKS
    )

    def column_side(p, carry):
        cp = c2_ref[p]
        cc = jnp.maximum(cp, 0)
        c12 = c1_ref[cc]
        j = p % COLS
        s = p // COLS
        h_ref[j, 0, s] = jnp.where(
            (cp >= 0) & (c12 >= 0), r1_ref[jnp.maximum(c12, 0)], 0.0
        )
        h_ref[j, 1, s] = jnp.where(cp >= 0, r2_ref[cc], 0.0)
        h_ref[j, 2, s] = r3_ref[p]
        return carry

    lax.fori_loop(0, BLOCKS, column_side, 0)


def pivot_kernel(c1_ref, c2_ref, k_ref, g_ref, r1_ref, r2_ref, r3_ref, s_ref):
    assemble(c1_ref, c2_ref, k_ref, r1_ref, r2_ref, r3_ref, s_ref, 12, 8, 4)
    g_ref[0:4] = r1_ref[0:4]
    g_ref[4:8] = r2_ref[0:4]
    g_ref[20:24] = r3_ref[0:4]
    for q in range(4):
        a = c1_ref[q]
        g_ref[8 + q] = jnp.where(a >= 0, r1_ref[jnp.maximum(a, 0)], 0.0)
        b = c2_ref[q]
        c = c1_ref[jnp.maximum(b, 0)]
        g_ref[12 + q] = jnp.where((b >= 0) & (c >= 0), r1_ref[jnp.maximum(c, 0)], 0.0)
        g_ref[16 + q] = jnp.where(b >= 0, r2_ref[jnp.maximum(b, 0)], 0.0)


def panels(c1, c2, k):
    return pl.pallas_call(
        panel_kernel,
        out_shape=[jax.ShapeDtypeStruct((BLOCKS, 4, 128), F32)] * 3
        + [jax.ShapeDtypeStruct((COLS, 3, TC, 4, 128), F32)],
        in_specs=[SMEM, SMEM, VMEM],
        out_specs=[VMEM] * 4,
        scratch_shapes=[pltpu.VMEM((BLOCKS, 8, 128), F32)],
        compiler_params=pltpu.CompilerParams(vmem_limit_bytes=32 << 20),
    )(c1, c2, k)


def pivots(c1, c2, k):
    return pl.pallas_call(
        pivot_kernel,
        out_shape=jax.ShapeDtypeStruct((24, 4, 128), F32),
        in_specs=[SMEM, SMEM, VMEM],
        out_specs=VMEM,
        scratch_shapes=[pltpu.VMEM((12, 4, 128), F32)]
        + [pltpu.VMEM((8, 4, 128), F32)] * 2
        + [pltpu.VMEM((8, 8, 128), F32)],
        compiler_params=pltpu.CompilerParams(vmem_limit_bytes=32 << 20),
    )(c1, c2, k)


def pack_kernel(a_ref, b_ref, o_ref):
    o_ref[:, 0, 0] = a_ref[0]
    o_ref[:, 1, 0] = b_ref[0]


def pack(a, b):
    block = pl.BlockSpec((1, TILE, TC, TILE), lambda t: (t, 0, 0, 0))
    return pl.pallas_call(
        pack_kernel,
        grid=(TR,),
        out_shape=jax.ShapeDtypeStruct((TILE, 2, TR, TC, TILE), F32),
        in_specs=[block, block],
        out_specs=pl.BlockSpec((TILE, 2, 1, TC, TILE), lambda t: (0, 0, t, 0, 0)),
        compiler_params=pltpu.CompilerParams(vmem_limit_bytes=32 << 20),
    )(a, b)


def extend_kernel(c1_ref, c2_ref, m1_ref, m2_ref, a_ref, o_ref, s_ref):
    def moved(src, m_ref, c):
        cc = jnp.maximum(c, 0)
        t = cc // ROWS
        i = cc % ROWS
        x = [src[i, j, t] for j in range(COLS)]
        x = x + [pltpu.roll(x[j], 7, 0) for j in range(MAXD)]
        out = []
        for j in range(COLS):
            acc = m_ref[0, j] * x[j]
            for d in range(1, MAXD + 1):
                acc = acc + m_ref[d, j] * x[j + d]
            out.append(jnp.where(c >= 0, acc, 0.0))
        return out

    def first(p, carry):
        got = moved(a_ref, m1_ref, c1_ref[p])
        t = p // ROWS
        i = p % ROWS
        for j in range(COLS):
            s_ref[i, j, t] = a_ref[i, j, TR + t] + got[j]
        return carry

    lax.fori_loop(0, BLOCKS, first, 0)

    def second(p, carry):
        got = moved(s_ref, m2_ref, c2_ref[p])
        t = p // ROWS
        i = p % ROWS
        for j in range(COLS):
            o_ref[i, j, t] = got[j]
        return carry

    lax.fori_loop(0, BLOCKS, second, 0)


def extended(c1, c2, m1, m2, a):
    smem = pl.BlockSpec(memory_space=pltpu.SMEM)
    vmem = pl.BlockSpec(memory_space=pltpu.VMEM)
    shape = (ROWS, COLS, TR, TC, 128)
    return pl.pallas_call(
        extend_kernel,
        out_shape=jax.ShapeDtypeStruct(shape, F32),
        in_specs=[smem, smem, vmem, vmem, vmem],
        out_specs=vmem,
        scratch_shapes=[pltpu.VMEM(shape, F32)],
        compiler_params=pltpu.CompilerParams(vmem_limit_bytes=32 << 20),
    )(c1, c2, m1, m2, a)


def dot(a, b):
    return jnp.dot(a, b, precision=HI, preferred_element_type=F32)


def dot_t(a, b, precision=HI):
    return lax.dot_general(
        a, b, (((1,), (1,)), ((), ())), precision=precision, preferred_element_type=F32
    )


def child_of(block_map):
    blocks = jnp.arange(BLOCKS, dtype=jnp.int32)
    hit = block_map[None, :] == blocks[:, None]
    ids = jnp.arange(block_map.shape[0], dtype=jnp.int32) + (PIVOTS // TILE + 1)
    return jnp.sum(jnp.where(hit, ids[None, :], 0), axis=1) - 1


def column_masks(child):
    blocks = jnp.arange(BLOCKS, dtype=jnp.int32)
    hits = jnp.stack([child == blocks + d for d in range(MAXD + 1)])
    hits = hits.reshape(MAXD + 1, TC, COLS).transpose(0, 2, 1).astype(F32)
    return jnp.broadcast_to(hits[..., None], (MAXD + 1, COLS, TC, 128))


def one_hot(child):
    return (child[:, None] == jnp.arange(BLOCKS, dtype=jnp.int32)[None, :]).astype(F32)


def own_rows(rows, later):
    n = rows.shape[0]
    half = PIVOTS // 2
    many = rows.reshape(n, TR, ROWS, 2, half).transpose(2, 3, 0, 1, 4)
    many = jnp.broadcast_to(many[:, None], (ROWS, COLS // 2, 2, n, TR, half))
    mine = lax.all_to_all(
        many.reshape(ROWS * COLS, n, TR, half), BOTH, 0, 0, tiled=True
    )
    mine, later = after(mine, later)
    other = lax.ppermute(mine, "col", [(j, j ^ 1) for j in range(COLS)])
    even = lax.axis_index("col") % 2 == 0
    halves = [jnp.where(even, mine, other), jnp.where(even, other, mine)]
    return jnp.concatenate(halves, axis=3).transpose(1, 2, 0, 3), later


def after(x, y):
    return lax.optimization_barrier((x, y))


def per_device(front_first, front_second, front_third, map_second, map_third):
    first = front_first.reshape(TR, TILE, TC, TILE)
    second = front_second.reshape(TR, TILE, TC, TILE)
    third = front_third.reshape(TR, TILE, TC, TILE)
    c1 = child_of(map_second)
    c2 = child_of(map_third)
    e1 = one_hot(c1)
    e2 = one_hot(c2)

    packed = jnp.concatenate([first[:, :, 0:2], second[:, :, 0:1], third[:, :, 0:1]], axis=2)
    packed = packed.transpose(1, 0, 2, 3)

    top = lax.all_to_all(packed[:, 0], BOTH, 0, 0, tiled=True)
    g = pivots(c1, c2, top.reshape(ROWS, COLS, 4, 128)).reshape(24, PIVOTS)
    packed, g = after(packed, g)
    pivot = lax.all_gather(g, BOTH, axis=1).reshape(6, PIVOTS, PIVOTS)

    packed = lax.all_to_all(packed.reshape(128, 16, 128), BOTH, 0, 0, tiled=True)
    r1, r2, r3, h = panels(c1, c2, packed.reshape(ROWS, COLS, 16, 128))
    r1, r2, r3 = (r.reshape(BLOCKS, PIVOTS) for r in (r1, r2, r3))
    cols = lax.all_to_all(h.reshape(COLS, 3, TC, PIVOTS), "col", 0, 0, tiled=True)
    cols = cols.transpose(1, 2, 0, 3)
    (first, second), cols = after((first, second), cols)
    moving = pack(first, second).reshape(TILE, 2 * TR, TC, TILE)
    (moving, cols), pivot = after((moving, cols), pivot)
    cols = lax.all_gather(cols, "row", axis=0)
    moving = lax.all_to_all(moving, BOTH, 0, 0, tiled=True)

    w1 = inverse_factor(pivot[0])
    lp1 = dot_t(pivot[2], w1)
    w2 = inverse_factor(pivot[1] - dot_t(lp1, lp1))
    lp1x = dot_t(pivot[3], w1)
    lp2 = dot_t(pivot[4] - dot_t(lp1x, lp1), w2)
    d3 = pivot[5] - dot_t(lp1x, lp1x) - dot_t(lp2, lp2)


    (moving, r1, r2, r3), w2 = after((moving, r1, r2, r3), w2)
    back = extended(
        c1,
        c2,
        column_masks(c1),
        column_masks(c2),
        moving.reshape(ROWS, COLS, 2 * TR, TC, TILE),
    )
    back, d3 = after(back, d3)
    back = lax.all_to_all(back.reshape(128, TR, TC, TILE), BOTH, 0, 0, tiled=True)
    w3 = inverse_factor(d3)

    l1 = dot_t(r1, w1)
    l1x = dot(e1, l1)
    l1xx = dot(e2, l1x)
    l2 = dot_t(r2 - dot_t(l1x, lp1), w2)
    l2x = dot(e2, l2)
    l3 = dot_t(r3 - dot_t(l1xx, lp1x) - dot_t(l2x, lp2), w3)
    (l1, l2, l3, cols), back = after((l1, l2, l3, cols), back)
    cols = cols.transpose(1, 2, 0, 3, 4).reshape(3, TC * TILE, PIVOTS)
    high = lax.Precision.HIGH
    l1c = dot_t(cols[0], w1, high)
    l2c = dot_t(cols[1] - dot_t(l1c, lp1, high), w2, high)
    l3c = cols[2] - dot_t(l1c, lp1x, high) - dot_t(l2c, lp2, high)
    l3c = dot_t(l3c, w3, high)
    rows, (l1, l2, l1c, l2c, l3c) = own_rows(
        jnp.stack([l1xx, l2x, l3]), (l1, l2, l1c, l2c, l3c)
    )
    rows = rows.reshape(3, TR * TILE, PIVOTS)
    l3r = rows[2]
    update = (
        dot_t(rows[0], l1c, high)
        + dot_t(rows[1], l2c, high)
        + dot_t(l3r, l3c, high)
    )
    assembled = third + back.transpose(1, 0, 2, 3)

    schur = assembled - update.reshape(TR, TILE, TC, TILE)
    pivot_blocks = PIVOTS // TILE
    row_keep = jnp.arange(TR) * ROWS + lax.axis_index("row") >= pivot_blocks
    col_keep = jnp.arange(TC) * COLS + lax.axis_index("col") >= pivot_blocks
    keep = row_keep[:, None, None, None] & col_keep[None, None, :, None]
    schur = jnp.where(keep, schur, 0.0)
    outer, schur = own_rows(jnp.stack([l1, l2]), schur)
    lower_first, lower_second = outer[0], outer[1]
    out = (1, TR, TILE, PIVOTS)
    return (
        lower_first.reshape(out),
        lower_second.reshape(out),
        l3r.reshape(out),
        schur.reshape(1, TR, TILE, 1, TC, TILE),
    )


def solution(mesh):
    front = P("row", None, None, "col", None, None)
    lower = P("row", None, None, None)
    return jax.shard_map(
        per_device,
        mesh=mesh,
        in_specs=(front, front, front, P(), P()),
        out_specs=(lower, lower, lower, front),
        check_vma=False,
    )
```
